32 devices in a mesh: grp: 2 (over y), seq: 4 (over z), wid: 2 (over x), rep: 2 (over core).
Axes of the slice: x: 2, y: 2, z: 4, core: 2. Of those that a mesh axis runs over, the one named last changes fastest.
Arguments:
- activations: bfloat16 [8192, 8192], P(('grp', 'seq'), ('wid', 'rep')), parts along dimension 0, may hold values from -6 to 6
- output_grads: bfloat16 [8192, 8192], P(('grp', 'seq'), ('wid', 'rep')), parts along dimension 0, may hold values from -6 to 6
- act_exponents: int32 [128, 64], P(('grp', 'seq'), ('wid', 'rep')), parts along dimension 0, may hold values from -2 to 2
- grad_exponents: int32 [128, 64], P(('grp', 'seq'), ('wid', 'rep')), parts along dimension 0, may hold values from -2 to 2
- input_blocks: bfloat16 [16, 128, 64], P(('wid', 'rep')), may hold values from -0.125 to 0.125
- input_index: int32 [16], P(('wid', 'rep')), may hold values from 0 to 63, as said below
- output_blocks: bfloat16 [16, 128, 64], P(('wid', 'rep')), may hold values from -0.125 to 0.125
- output_index: int32 [16], P(('wid', 'rep')), may hold values from 0 to 63, as said below
- fisher_inverse: float32 [4096, 4096], P('seq', 'wid'), may hold values from -1 to 7, as said below
Outputs:
- preconditioned: float32 [64, 2, 4096], P(('grp', 'wid'), 'rep', 'seq'), parts along dimension 0
The draws below stay inside these ranges and needn't reach their ends.
There are 2 independent parts, one for each index of `grp`. The reference program is written for one: setup_inputs(seed, part) draws one part's arguments, and reference() takes and returns one part's arrays. A program takes and returns all parts, laid end to end along the dimension named above; an argument that names none is the same for every part. Nothing has to cross between parts.
Inputs may be any that keep to these rules, and one draw needn't show every extreme that they name: `input_index`: Rising; exactly one index in each aligned run of 4 blocks; the first block and the last block are always named. `output_index`: Rising; exactly one index in each aligned run of 4 blocks; the first block and the last block are always named. `fisher_inverse`: Symmetric.
All inputs are finite; a program needn't handle non-finite values.
Results may differ from the reference program's by a relative error of at most 0.00045.
Values sent between devices are 32-bit elements; how exact they have to be, the bound alone decides.
A program may use at most 64 MiB of HBM per device.

```python
import jax
import jax.numpy as jnp
from jax import lax

D = 8192
R = 64
BLK = 128
BGROUP = 4
LEN = 64
NBLK = 64
NSEL = 16
Q = 4096
SEQS = 64
TOKENS = 4096
N_REP = 2


def block_choice(key):
    offsets = jax.random.randint(key, (NSEL,), 0, BGROUP)
    offsets = offsets.at[0].set(0).at[NSEL - 1].set(BGROUP - 1)
    return (jnp.arange(NSEL) * BGROUP + offsets).astype(jnp.int32)


def draw_input_index(key, part):
    return block_choice(jax.random.fold_in(key, 3))


def draw_output_index(key, part):
    return block_choice(jax.random.fold_in(key, 7))


def draw_fisher_inverse(key, part):
    key_diag, key_off = jax.random.split(jax.random.fold_in(key, 11))
    diagonal = jnp.exp(jax.random.uniform(key_diag, (Q,), jnp.float32, 0.0, 1.3862944))
    noise = jax.random.normal(key_off, (Q, Q), jnp.float32) * (0.4 / Q ** 0.5)
    offdiag = (noise + noise.T) * 0.5 ** 0.5
    return (offdiag + jnp.diag(diagonal)).astype(jnp.float32)


def with_ends(values, key, low, largest):
    shape = values.shape
    spot = [jax.random.randint(jax.random.fold_in(key, axis), (), 0, shape[axis]) for axis in range(len(shape))]
    values = values.at[tuple(spot)].set(low)
    longest = shape.index(max(shape))
    spot[longest] = (spot[longest] + 1) % shape[longest]
    return values.at[tuple(spot)].set(largest)


def level_of(stream_key, shape, cuts, smallest, top_value):
    gain = 1.0
    for axis_at, blocks in cuts:
        draws = jax.random.uniform(jax.random.fold_in(jax.random.fold_in(stream_key, 6), axis_at), (blocks,), jnp.float32, smallest / len(cuts), top_value / len(cuts))
        gain = gain * jnp.repeat(jnp.exp(draws), shape[axis_at] // blocks).reshape((-1,) + (1,) * (len(shape) - 1 - axis_at))
    return gain


def bell_draw(key, extent, width, limit, pieces=(), kind=jnp.bfloat16):
    array = width * jax.random.normal(key, extent, jnp.float32)
    if pieces:
        array = array * level_of(key, extent, pieces, -0.22, 0.18)
    return jnp.clip(array, -limit, limit).astype(kind)


def setup_inputs(seed: int = 0, part: int = 0) -> dict:
    arg_keys = jax.random.split(jax.random.key(seed), 10)
    own_keys = jax.random.split(jax.random.fold_in(arg_keys[9], part), 10)
    activations = bell_draw(own_keys[0], (TOKENS, D), 1.0, 6.0, ((0, 4), (1, 4)))
    output_grads = bell_draw(own_keys[1], (TOKENS, D), 1.0, 6.0, ((0, 4), (1, 4)))
    act_exponents = with_ends(jax.random.randint(own_keys[2], (SEQS, NBLK), -2, 3), jax.random.fold_in(own_keys[2], 1), -2, 2).astype(jnp.int32)
    grad_exponents = with_ends(jax.random.randint(own_keys[3], (SEQS, NBLK), -2, 3), jax.random.fold_in(own_keys[3], 1), -2, 2).astype(jnp.int32)
    input_blocks = bell_draw(arg_keys[4], (NSEL, BLK, R), (NSEL * BLK) ** -0.5, 0.125, ((0, 4),))
    input_index = draw_input_index(jax.random.fold_in(arg_keys[9], 71), part)
    output_blocks = bell_draw(arg_keys[6], (NSEL, BLK, R), (NSEL * BLK) ** -0.5, 0.125, ((0, 4),))
    output_index = draw_output_index(jax.random.fold_in(arg_keys[9], 71), part)
    fisher_inverse = draw_fisher_inverse(jax.random.fold_in(arg_keys[9], 71), part)
    return dict(activations=activations, output_grads=output_grads, act_exponents=act_exponents, grad_exponents=grad_exponents, input_blocks=input_blocks, input_index=input_index, output_blocks=output_blocks, output_index=output_index, fisher_inverse=fisher_inverse)


def select_blocks(values, exponents, index):
    seq_count = values.shape[0] // LEN
    blocks = values.reshape(seq_count, LEN, NBLK, BLK)
    picked = jnp.take(blocks, index, axis=2)
    scaling = jnp.exp2(jnp.take(exponents, index, axis=1).astype(jnp.float32)).astype(jnp.bfloat16)
    return (picked * scaling[:, None, :, None]).reshape(values.shape[0], NSEL * BLK)


def reference(activations, output_grads, act_exponents, grad_exponents, input_blocks, input_index, output_blocks, output_index, fisher_inverse):
    act_proj = jnp.dot(select_blocks(activations, act_exponents, input_index), input_blocks.reshape(NSEL * BLK, R), preferred_element_type=jnp.float32)
    grad_proj = jnp.dot(select_blocks(output_grads, grad_exponents, output_index), output_blocks.reshape(NSEL * BLK, R), preferred_element_type=jnp.float32)
    outer = jnp.einsum("sti,stj->sij", grad_proj.reshape(SEQS, LEN, R), act_proj.reshape(SEQS, LEN, R), precision=lax.Precision.HIGHEST) / LEN
    flat = outer.reshape(SEQS, Q)
    result = lax.dot_general(flat, fisher_inverse, (((1,), (1,)), ((), ())), precision=lax.Precision.HIGHEST, preferred_element_type=jnp.float32)
    return result.reshape(SEQS // N_REP, N_REP, Q)
```

```python
import functools

import jax
import jax.numpy as jnp
from jax import lax
from jax.experimental import pallas as pl
from jax.experimental.pallas import tpu as pltpu
from jax.sharding import PartitionSpec as P

BLK = 128
LEN = 64
MESH = pl.DeviceIdType.MESH
NT = (((1,), (1,)), ((), ()))


def split(value):
    high = value.astype(jnp.bfloat16)
    low = (value - high.astype(jnp.float32)).astype(jnp.bfloat16)
    return high, low


def project_kernel(
    rep_count,
    block_count,
    act_index,
    grad_index,
    act_exp,
    grad_exp,
    act_blocks,
    grad_blocks,
    acts,
    grads,
    out,
    held,
    sems,
):
    chosen = act_blocks.shape[0]
    width = act_blocks.shape[1]
    seqs = act_exp.shape[0]
    per_rep = seqs // rep_count
    sides = ((grad_index, grad_exp, grad_blocks, grads), (act_index, act_exp, act_blocks, acts))
    copies = []
    for side, (index, _, _, values) in enumerate(sides):
        for b in range(chosen):
            at = pl.multiple_of(lax.rem(index[b], block_count) * BLK, BLK)
            copy = pltpu.make_async_copy(
                values.at[:, pl.ds(at, BLK)], held.at[side, b], sems.at[side, b]
            )
            copy.start()
            copies.append(copy)
    for side, (index, exps, blocks, _) in enumerate(sides):
        scaled = [[] for _ in range(rep_count)]
        for b in range(chosen):
            copies[side * chosen + b].wait()
            local = lax.rem(index[b], block_count)
            for k in range(rep_count):
                rows = []
                for l in range(per_rep):
                    s = l * rep_count + k
                    power = jnp.exp2(jnp.full((LEN, BLK), exps[s, local], jnp.int32).astype(jnp.float32))
                    rows.append(held[side, b, pl.ds(s * LEN, LEN), :] * power.astype(jnp.bfloat16))
                scaled[k].append(jnp.concatenate(rows, axis=0))
        weight = jnp.concatenate([blocks[b] for b in range(chosen)], axis=1)
        for k in range(rep_count):
            out[k, pl.ds(side * width, width), :] = lax.dot_general(
                weight, jnp.concatenate(scaled[k], axis=1), NT, preferred_element_type=jnp.float32
            )


def main_kernel(
    counts,
    proj,
    fisher,
    out,
    rep_in,
    summed,
    wid_in,
    outers,
    fisher_f32,
    fisher_high,
    fisher_low,
    partial_value,
    result_in,
    fisher_sems,
    rep_sems,
    wid_sems,
    seq_sems,
    result_sems,
):
    seq_count, wid_count, rep_count = counts
    q = lax.axis_index("seq")
    w = lax.axis_index("wid")
    r = lax.axis_index("rep")
    width = proj.shape[1] // 2
    tokens = proj.shape[2]
    slice_rows = width // wid_count
    pairs = slice_rows // 2
    per_rep = tokens // LEN
    fisher_rows = fisher.shape[0]
    parts = fisher_sems.shape[0]
    part_rows = fisher_rows // parts

    fisher_copies = []
    for f in range(parts):
        rows = pl.ds(f * part_rows, part_rows)
        copy = pltpu.make_async_copy(fisher.at[rows, :], fisher_f32.at[rows, :], fisher_sems.at[f])
        copy.start()
        fisher_copies.append(copy)

    peers = (
        [{"rep": lax.rem(r + d, rep_count)} for d in range(1, rep_count)]
        + [{"wid": lax.rem(w + d, wid_count)} for d in range(1, wid_count)]
        + [{"seq": lax.rem(q + d, seq_count)} for d in range(1, seq_count)]
    )
    barrier = pltpu.get_barrier_semaphore()
    for peer in peers:
        pl.semaphore_signal(barrier, inc=1, device_id=peer, device_id_type=MESH)
    pl.semaphore_wait(barrier, len(peers))

    def send(src, dst, sems, slot, peer):
        copy = pltpu.make_async_remote_copy(
            src_ref=src,
            dst_ref=dst,
            send_sem=sems.at[0, slot],
            recv_sem=sems.at[1, slot],
            device_id=peer,
            device_id_type=MESH,
        )
        copy.start()
        return copy

    rep_copies = []
    for d in range(1, rep_count):
        to = lax.rem(r + d, rep_count)
        rep_copies.append(send(proj.at[to], rep_in.at[d - 1], rep_sems, d - 1, {"rep": to}))
    for copy in rep_copies:
        copy.wait_recv()
    total = proj[r]
    for d in range(1, rep_count):
        total = total + rep_in[d - 1]
    summed[...] = total

    wid_copies = []
    for d in range(1, wid_count):
        to = lax.rem(w + d, wid_count)
        wid_copies.append(
            send(
                summed.at[pl.ds(width, width), :],
                wid_in.at[d - 1, pl.ds(0, width), :],
                wid_sems,
                2 * d - 2,
                {"wid": to},
            )
        )
        wid_copies.append(
            send(
                summed.at[pl.ds(pl.multiple_of(to * slice_rows, 8), slice_rows), :],
                wid_in.at[d - 1, pl.ds(width, slice_rows), :],
                wid_sems,
                2 * d - 1,
                {"wid": to},
            )
        )

    for f in range(parts):
        fisher_copies[f].wait()

        @pl.loop(0, part_rows // 32)
        def _(step):
            rows = pl.ds(pl.multiple_of(f * part_rows + step * 32, 32), 32)
            high, low = split(fisher_f32[rows, :])
            fisher_high[rows, :] = high
            fisher_low[rows, :] = low

    for copy in wid_copies:
        copy.wait_recv()
    act = summed[pl.ds(width, width), :]
    grad = summed[pl.ds(pl.multiple_of(w * slice_rows, 8), slice_rows), :]
    for d in range(1, wid_count):
        act = act + wid_in[d - 1, pl.ds(0, width), :]
        grad = grad + wid_in[d - 1, pl.ds(width, slice_rows), :]
    act_high, act_low = split(act)
    grad = grad * (1.0 / LEN)
    grad_high = grad.astype(jnp.bfloat16).astype(jnp.float32)
    grad_low = grad - grad_high
    own = lax.broadcasted_iota(jnp.int32, (per_rep, tokens), 1) // LEN == lax.broadcasted_iota(
        jnp.int32, (per_rep, tokens), 0
    )

    def spread(rows_of, first):
        rows = []
        for i in range(first, slice_rows, 2):
            row = jnp.broadcast_to(rows_of[i : i + 1, :], (per_rep, tokens))
            rows.append(jnp.where(own, row, 0.0))
        return jnp.concatenate(rows, axis=0).astype(jnp.bfloat16)

    halves = []
    for first in range(2):
        high = spread(grad_high, first)
        low = spread(grad_low, first)
        halves.append(
            lax.dot_general(high, act_high, NT, preferred_element_type=jnp.float32)
            + (
                lax.dot_general(low, act_high, NT, preferred_element_type=jnp.float32)
                + lax.dot_general(high, act_low, NT, preferred_element_type=jnp.float32)
            )
        )
    outers[q] = jnp.concatenate(halves, axis=1).reshape(pairs, per_rep, 2 * width)

    seq_copies = []
    for d in range(1, seq_count):
        to = lax.rem(q + d, seq_count)
        seq_copies.append(send(outers.at[q], outers.at[q], seq_sems, d - 1, {"seq": to}))
    for copy in seq_copies:
        copy.wait_recv()

    rows = seq_count * per_rep
    flat = jnp.concatenate([outers[:, p].reshape(rows, 2 * width) for p in range(pairs)], axis=1)
    flat_high, flat_low = split(flat)
    both = jnp.concatenate([flat_high, flat_low], axis=0)
    own_rows = rows // wid_count
    tile = min(fisher_rows, 256)
    for t in range(fisher_rows // tile):
        at = pl.ds(t * tile, tile)
        first = lax.dot_general(fisher_high[at, :], both, NT, preferred_element_type=jnp.float32)
        second = lax.dot_general(fisher_low[at, :], flat_high, NT, preferred_element_type=jnp.float32)
        first = first.T
        value = first[:rows, :] + (first[rows:, :] + second.T)
        partial_value[:, :, at] = value.reshape(wid_count, own_rows, tile)

    result_copies = []
    for d in range(1, wid_count):
        to = lax.rem(w + d, wid_count)
        result_copies.append(
            send(partial_value.at[to], result_in.at[d - 1], result_sems, d - 1, {"wid": to})
        )
    for copy in result_copies:
        copy.wait_recv()
    value = partial_value[w]
    for d in range(1, wid_count):
        value = value + result_in[d - 1]
    out[...] = value.reshape(own_rows, 1, fisher_rows)
    for copy in rep_copies + wid_copies + seq_copies + result_copies:
        copy.wait_send()


def shards(
    activations,
    output_grads,
    act_exponents,
    grad_exponents,
    input_blocks,
    input_index,
    output_blocks,
    output_index,
    fisher_inverse,
):
    seq_count = lax.axis_size("seq")
    wid_count = lax.axis_size("wid")
    rep_count = lax.axis_size("rep")
    chosen, _, width = input_blocks.shape
    tok_rows = activations.shape[0]
    block_count = activations.shape[1] // BLK
    tokens = tok_rows // rep_count
    per_rep = tokens // LEN
    slice_rows = width // wid_count
    rows = seq_count * per_rep
    own_rows = rows // wid_count
    fisher_rows, fisher_cols = fisher_inverse.shape
    vmem = pl.BlockSpec(memory_space=pltpu.VMEM)
    smem = pl.BlockSpec(memory_space=pltpu.SMEM)
    hbm = pl.BlockSpec(memory_space=pltpu.HBM)
    f32 = jnp.float32
    dma = pltpu.SemaphoreType.DMA
    projected = pl.pallas_call(
        functools.partial(project_kernel, rep_count, block_count),
        out_shape=jax.ShapeDtypeStruct((rep_count, 2 * width, tokens), f32),
        in_specs=[smem, smem, smem, smem, vmem, vmem, hbm, hbm],
        out_specs=vmem,
        scratch_shapes=[pltpu.VMEM((2, chosen, tok_rows, BLK), jnp.bfloat16), dma((2, chosen))],
        compiler_params=pltpu.CompilerParams(vmem_limit_bytes=56 << 20),
        name="project",
    )(
        input_index,
        output_index,
        act_exponents,
        grad_exponents,
        jnp.swapaxes(input_blocks, 1, 2),
        jnp.swapaxes(output_blocks, 1, 2),
        activations,
        output_grads,
    )
    return pl.pallas_call(
        functools.partial(main_kernel, (seq_count, wid_count, rep_count)),
        out_shape=jax.ShapeDtypeStruct((own_rows, 1, fisher_rows), f32),
        in_specs=[vmem, hbm],
        out_specs=vmem,
        scratch_shapes=[
            pltpu.VMEM((rep_count - 1, 2 * width, tokens), f32),
            pltpu.VMEM((2 * width, tokens), f32),
            pltpu.VMEM((wid_count - 1, width + slice_rows, tokens), f32),
            pltpu.VMEM((seq_count, slice_rows // 2, per_rep, 2 * width), f32),
            pltpu.VMEM((fisher_rows, fisher_cols), f32),
            pltpu.VMEM((fisher_rows, fisher_cols), jnp.bfloat16),
            pltpu.VMEM((fisher_rows, fisher_cols), jnp.bfloat16),
            pltpu.VMEM((wid_count, own_rows, fisher_rows), f32),
            pltpu.VMEM((wid_count - 1, own_rows, fisher_rows), f32),
            dma((4,)),
            dma((2, rep_count - 1)),
            dma((2, 2 * (wid_count - 1))),
            dma((2, seq_count - 1)),
            dma((2, wid_count - 1)),
        ],
        compiler_params=pltpu.CompilerParams(
            collective_id=0, has_side_effects=True, vmem_limit_bytes=56 << 20
        ),
        name="exchange",
    )(projected, fisher_inverse)


def solution(mesh):
    placed = (
        P(("grp", "seq"), ("wid", "rep")),
        P(("grp", "seq"), ("wid", "rep")),
        P(("grp", "seq"), ("wid", "rep")),
        P(("grp", "seq"), ("wid", "rep")),
        P(("wid", "rep"), None, None),
        P(("wid", "rep")),
        P(("wid", "rep"), None, None),
        P(("wid", "rep")),
        P("seq", "wid"),
    )
    return jax.shard_map(
        shards,
        mesh=mesh,
        in_specs=placed,
        out_specs=P(("grp", "wid"), "rep", "seq"),
        check_vma=False,
    )
```

```python
import functools

import jax
import jax.numpy as jnp
from jax import lax
from jax.experimental import pallas as pl
from jax.experimental.pallas import tpu as pltpu
from jax.sharding import PartitionSpec as P

BLK = 128
LEN = 64
MESH = pl.DeviceIdType.MESH
NT = (((1,), (1,)), ((), ()))


def split(value):
    high = value.astype(jnp.bfloat16)
    low = (value - high.astype(jnp.float32)).astype(jnp.bfloat16)
    return high, low


def kernel(
    counts,
    chunks,
    act_index,
    grad_index,
    act_exp,
    grad_exp,
    act_blocks,
    grad_blocks,
    acts,
    grads,
    fisher,
    out,
    held,
    proj,
    rep_in,
    summed,
    wid_in,
    outers,
    flat,
    fisher_f32,
    fisher_high,
    fisher_low,
    partial_value,
    result_in,
    held_sems,
    fisher_sems,
    rep_sems,
    wid_sems,
    seq_sems,
    result_sems,
):
    seq_count, wid_count, rep_count = counts
    q = lax.axis_index("seq")
    w = lax.axis_index("wid")
    r = lax.axis_index("rep")
    chosen, width, _ = act_blocks.shape
    block_count = acts.shape[1] // BLK
    seqs = act_exp.shape[0]
    per_rep = seqs // rep_count
    chunk_seqs = per_rep // chunks
    tokens = chunk_seqs * LEN
    slice_rows = width // wid_count
    pairs = slice_rows // 2
    fisher_rows = fisher.shape[0]
    parts = fisher_sems.shape[0]
    part_rows = fisher_rows // parts
    rows = seq_count * per_rep
    own_rows = rows // wid_count
    tiles, _, _, tile = partial_value.shape

    peers = (
        [{"rep": lax.rem(r + d, rep_count)} for d in range(1, rep_count)]
        + [{"wid": lax.rem(w + d, wid_count)} for d in range(1, wid_count)]
        + [{"seq": lax.rem(q + d, seq_count)} for d in range(1, seq_count)]
    )
    barrier = pltpu.get_barrier_semaphore()
    for peer in peers:
        pl.semaphore_signal(barrier, inc=1, device_id=peer, device_id_type=MESH)

    sides = ((grad_index, grad_exp, grad_blocks, grads), (act_index, act_exp, act_blocks, acts))
    held_copies = []
    for c in range(chunks):
        span = pl.ds(c * rep_count * tokens, rep_count * tokens)
        for side in range(2):
            for b in range(block_count):
                copy = pltpu.make_async_copy(
                    sides[side][3].at[span, pl.ds(b * BLK, BLK)],
                    held[2 * c + side].at[b],
                    held_sems.at[c, side, b],
                )
                copy.start()
                held_copies.append(copy)
    fisher_copies = []
    for f in range(parts):
        span = pl.ds(f * part_rows, part_rows)
        copy = pltpu.make_async_copy(fisher.at[span, :], fisher_f32.at[span, :], fisher_sems.at[f])
        copy.start()
        fisher_copies.append(copy)

    def send(src, dst, sems, slot, peer):
        copy = pltpu.make_async_remote_copy(
            src_ref=src,
            dst_ref=dst,
            send_sem=sems.at[(0, *slot)],
            recv_sem=sems.at[(1, *slot)],
            device_id=peer,
            device_id_type=MESH,
        )
        copy.start()
        return copy

    def project(c):
        for side, (index, exps, blocks, _) in enumerate(sides):
            for b in range(block_count):
                held_copies[(2 * c + side) * block_count + b].wait()
            scaled = [[] for _ in range(rep_count)]
            for b in range(chosen):
                local = lax.rem(index[b], block_count)
                for k in range(rep_count):
                    pieces = []
                    for l in range(chunk_seqs):
                        s = l * rep_count + k
                        exponent = exps[c * chunk_seqs * rep_count + s, local]
                        power = jnp.exp2(jnp.full((LEN, BLK), exponent, jnp.int32).astype(jnp.float32))
                        values = held[2 * c + side][local, pl.ds(s * LEN, LEN), :]
                        pieces.append(values * power.astype(jnp.bfloat16))
                    scaled[k].append(jnp.concatenate(pieces, axis=0))
            weight = jnp.concatenate([blocks[b] for b in range(chosen)], axis=1)
            for k in range(rep_count):
                proj[c, k, pl.ds(side * width, width), :] = lax.dot_general(
                    weight,
                    jnp.concatenate(scaled[k], axis=1),
                    NT,
                    preferred_element_type=jnp.float32,
                )

    def split_fisher(f):
        fisher_copies[f].wait()

        @pl.loop(0, part_rows // 32)
        def _(step):
            span = pl.ds(pl.multiple_of(f * part_rows + step * 32, 32), 32)
            high, low = split(fisher_f32[span, :])
            fisher_high[span, :] = high
            fisher_low[span, :] = low

    rep_copies = [[] for _ in range(chunks)]
    for c in range(chunks):
        project(c)
        if c == 0:
            pl.semaphore_wait(barrier, len(peers))
        for d in range(1, rep_count):
            to = lax.rem(r + d, rep_count)
            rep_copies[c].append(
                send(proj.at[c, to], rep_in.at[d - 1, c], rep_sems, (d - 1, c), {"rep": to})
            )

    wid_copies = [[] for _ in range(chunks)]
    for c in range(chunks):
        for copy in rep_copies[c]:
            copy.wait_recv()
        total = proj[c, r]
        for d in range(1, rep_count):
            total = total + rep_in[d - 1, c]
        summed[c] = total
        for d in range(1, wid_count):
            to = lax.rem(w + d, wid_count)
            wid_copies[c].append(
                send(
                    summed.at[c, pl.ds(width, width), :],
                    wid_in.at[d - 1, c, pl.ds(0, width), :],
                    wid_sems,
                    (2 * d - 2, c),
                    {"wid": to},
                )
            )
            wid_copies[c].append(
                send(
                    summed.at[c, pl.ds(pl.multiple_of(to * slice_rows, 8), slice_rows), :],
                    wid_in.at[d - 1, c, pl.ds(width, slice_rows), :],
                    wid_sems,
                    (2 * d - 1, c),
                    {"wid": to},
                )
            )

    for f in range(parts // 2):
        split_fisher(f)

    row = lax.broadcasted_iota(jnp.int32, (8, tokens), 0)
    own = lax.broadcasted_iota(jnp.int32, (8, tokens), 1) // LEN == row % chunk_seqs
    group = 8 // chunk_seqs

    def spread(rows_of, first):
        pieces = []
        for p in range(0, pairs, group):
            value = jnp.broadcast_to(rows_of[2 * p + first : 2 * p + first + 1, :], (8, tokens))
            for j in range(1, group):
                i = 2 * (p + j) + first
                value = jnp.where(
                    row // chunk_seqs == j, jnp.broadcast_to(rows_of[i : i + 1, :], (8, tokens)), value
                )
            pieces.append(jnp.where(own, value, 0.0))
        return jnp.concatenate(pieces, axis=0).astype(jnp.bfloat16)

    seq_copies = [[] for _ in range(chunks)]
    for c in range(chunks):
        for copy in wid_copies[c]:
            copy.wait_recv()
        act = summed[c, pl.ds(width, width), :]
        grad = summed[c, pl.ds(pl.multiple_of(w * slice_rows, 8), slice_rows), :]
        for d in range(1, wid_count):
            act = act + wid_in[d - 1, c, pl.ds(0, width), :]
            grad = grad + wid_in[d - 1, c, pl.ds(width, slice_rows), :]
        act_high, act_low = split(act)
        grad = grad * (1.0 / LEN)
        grad_high = grad.astype(jnp.bfloat16).astype(jnp.float32)
        grad_low = grad - grad_high
        halves = []
        for first in range(2):
            high = spread(grad_high, first)
            low = spread(grad_low, first)
            halves.append(
                lax.dot_general(high, act_high, NT, preferred_element_type=jnp.float32)
                + (
                    lax.dot_general(low, act_high, NT, preferred_element_type=jnp.float32)
                    + lax.dot_general(high, act_low, NT, preferred_element_type=jnp.float32)
                )
            )
        outers[q, c] = jnp.concatenate(halves, axis=1)
        for d in range(1, seq_count):
            to = lax.rem(q + d, seq_count)
            seq_copies[c].append(
                send(outers.at[q, c], outers.at[q, c], seq_sems, (d - 1, c), {"seq": to})
            )

    for f in range(parts // 2, parts):
        split_fisher(f)

    for c in range(chunks):
        for copy in seq_copies[c]:
            copy.wait_recv()
        for o in range(seq_count):
            for p in range(pairs):
                flat[pl.ds(o * per_rep + c * chunk_seqs, chunk_seqs), pl.ds(p * BLK, BLK)] = outers[
                    o, c, pl.ds(p * chunk_seqs, chunk_seqs), :
                ]

    flat_high, flat_low = split(flat[...])
    both = jnp.concatenate([flat_high, flat_low], axis=0)
    result_copies = []
    for t in range(tiles):
        at = pl.ds(t * tile, tile)
        first = lax.dot_general(fisher_high[at, :], both, NT, preferred_element_type=jnp.float32)
        second = lax.dot_general(fisher_low[at, :], flat_high, NT, preferred_element_type=jnp.float32)
        first = first.T
        value = first[:rows, :] + (first[rows:, :] + second.T)
        partial_value[t] = value.reshape(wid_count, own_rows, tile)
        for d in range(1, wid_count):
            to = lax.rem(w + d, wid_count)
            result_copies.append(
                send(
                    partial_value.at[t, to],
                    result_in.at[d - 1, t],
                    result_sems,
                    (d - 1, t),
                    {"wid": to},
                )
            )
    for copy in result_copies:
        copy.wait_recv()
    for t in range(tiles):
        value = partial_value[t, w]
        for d in range(1, wid_count):
            value = value + result_in[d - 1, t]
        out[:, :, pl.ds(t * tile, tile)] = value.reshape(own_rows, 1, tile)
    for copies in rep_copies + wid_copies + seq_copies + [result_copies]:
        for copy in copies:
            copy.wait_send()


def shards(
    activations,
    output_grads,
    act_exponents,
    grad_exponents,
    input_blocks,
    input_index,
    output_blocks,
    output_index,
    fisher_inverse,
):
    seq_count = lax.axis_size("seq")
    wid_count = lax.axis_size("wid")
    rep_count = lax.axis_size("rep")
    chunks = 2
    width = input_blocks.shape[2]
    tok_rows, features = activations.shape
    per_rep = tok_rows // LEN // rep_count
    tokens = per_rep // chunks * LEN
    slice_rows = width // wid_count
    pairs = slice_rows // 2
    rows = seq_count * per_rep
    own_rows = rows // wid_count
    fisher_rows, fisher_cols = fisher_inverse.shape
    tile = min(fisher_rows, 256)
    tiles = fisher_rows // tile
    parts = 4
    vmem = pl.BlockSpec(memory_space=pltpu.VMEM)
    smem = pl.BlockSpec(memory_space=pltpu.SMEM)
    hbm = pl.BlockSpec(memory_space=pltpu.HBM)
    f32 = jnp.float32
    dma = pltpu.SemaphoreType.DMA
    return pl.pallas_call(
        functools.partial(kernel, (seq_count, wid_count, rep_count), chunks),
        out_shape=jax.ShapeDtypeStruct((own_rows, 1, fisher_rows), f32),
        in_specs=[smem, smem, smem, smem, vmem, vmem, hbm, hbm, hbm],
        out_specs=vmem,
        scratch_shapes=[
            [pltpu.VMEM((features // BLK, tok_rows // chunks, BLK), jnp.bfloat16)] * (2 * chunks),
            pltpu.VMEM((chunks, rep_count, 2 * width, tokens), f32),
            pltpu.VMEM((rep_count - 1, chunks, 2 * width, tokens), f32),
            pltpu.VMEM((chunks, 2 * width, tokens), f32),
            pltpu.VMEM((wid_count - 1, chunks, width + slice_rows, tokens), f32),
            pltpu.VMEM((seq_count, chunks, pairs * per_rep // chunks, 2 * width), f32),
            pltpu.VMEM((rows, pairs * 2 * width), f32),
            pltpu.VMEM((fisher_rows, fisher_cols), f32),
            pltpu.VMEM((fisher_rows, fisher_cols), jnp.bfloat16),
            pltpu.VMEM((fisher_rows, fisher_cols), jnp.bfloat16),
            pltpu.VMEM((tiles, wid_count, own_rows, tile), f32),
            pltpu.VMEM((wid_count - 1, tiles, own_rows, tile), f32),
            dma((chunks, 2, features // BLK)),
            dma((parts,)),
            dma((2, rep_count - 1, chunks)),
            dma((2, 2 * (wid_count - 1), chunks)),
            dma((2, seq_count - 1, chunks)),
            dma((2, wid_count - 1, tiles)),
        ],
        compiler_params=pltpu.CompilerParams(
            collective_id=0, has_side_effects=True, vmem_limit_bytes=56 << 20
        ),
        name="exchange",
    )(
        input_index,
        output_index,
        act_exponents,
        grad_exponents,
        jnp.swapaxes(input_blocks, 1, 2),
        jnp.swapaxes(output_blocks, 1, 2),
        activations,
        output_grads,
        fisher_inverse,
    )


def solution(mesh):
    placed = (
        P(("grp", "seq"), ("wid", "rep")),
        P(("grp", "seq"), ("wid", "rep")),
        P(("grp", "seq"), ("wid", "rep")),
        P(("grp", "seq"), ("wid", "rep")),
        P(("wid", "rep"), None, None),
        P(("wid", "rep")),
        P(("wid", "rep"), None, None),
        P(("wid", "rep")),
        P("seq", "wid"),
    )
    return jax.shard_map(
        shards,
        mesh=mesh,
        in_specs=placed,
        out_specs=P(("grp", "wid"), "rep", "seq"),
        check_vma=False,
    )
```
